512 devices in a mesh: tile: 32 (over z, core), help: 4 (over x), dp: 4 (over y).
Axes of the slice: x: 4, y: 4, z: 16, core: 2. Of those that a mesh axis runs over, the one named last changes fastest.
Arguments:
- tokens: bfloat16 [4, 262144, 256], P('dp', ('tile', 'help')), may hold values from -6 to 6
- d_out: bfloat16 [4, 262144, 256], P('dp', ('tile', 'help')), may hold values from -6 to 6
- gain: float32 [256], replicated, may hold values from 0.5 to 1.5
- w_qkv: bfloat16 [256, 768], replicated, may hold values from -10 to 10
- w_out: bfloat16 [256, 256], replicated, may hold values from -0.375 to 0.375
- counts: int32 [4, 1024], P('dp', 'tile'), may hold values from 0 to 256, as said below
Outputs:
- grad_tokens: bfloat16 [4, 262144, 256], P('dp', ('tile', 'help'))
- grad_qkv: float32 [256, 768], replicated
- grad_out: float32 [256, 256], replicated
- grad_gain: float32 [256], replicated
The draws below stay inside these ranges and needn't reach their ends.
Inputs may be any that keep to these rules, and one draw needn't show every extreme that they name: `counts`: entry s * 8 + w of a slab, with s = tile index * 4 + help index, is the active voxel count of window slot w of device s. A device's active windows come first. Of the two devices of a tile whose help indices differ by 2, one holds 8 active windows and the other 4. Every active window holds 1 to 256 voxels, and some window is full in every draw.
All inputs are finite; a program needn't handle non-finite values.
Results may differ from the reference program's by a relative error of at most 0.005.
The reference program's roundings to bfloat16 on the way count: a program that leaves them out, or rounds other values in their place, can miss the bound.
Values may be sent and summed in bfloat16 or wider, within the bound.
No kernel may reach another device: no remote copies, remote signals or barrier semaphores. Data moves between devices by JAX's collectives and lax.ppermute only.
A program may use at most 64 MiB of HBM per device.

```python
import math
import jax
import jax.numpy as jnp
from jax import lax

D = 256
HEADS = 8
WIN = 256
WKEEP = 6
MOVE = 2
SLAB_SLOTS = 262144
N_TILE = 32
N_HELP = 4
N_DP = 4


def draw_counts(key, part):
    slot_count = WKEEP + MOVE
    first_key = jax.random.fold_in(key, 11)
    second_key = jax.random.fold_in(key, 12)
    coin_flip = jax.random.randint(first_key, (N_DP, N_TILE, N_HELP), 0, 2)
    help_ids = jnp.arange(N_HELP, dtype=jnp.int32)
    upper_bit = help_ids // 2 % 2
    pair_base = help_ids - 2 * upper_bit
    crowded = (coin_flip[:, :, pair_base] + upper_bit[None, None, :]) % 2
    active_windows = jnp.where(crowded == 1, WKEEP + MOVE, WKEEP - MOVE)
    voxel_counts = jax.random.randint(second_key, (N_DP, N_TILE, N_HELP, slot_count), 1, WIN + 1)
    voxel_counts = voxel_counts.at[:, 0, 0, 0].set(WIN)
    window_ids = jnp.arange(slot_count, dtype=jnp.int32)
    result = jnp.where(window_ids[None, None, None, :] < active_windows[:, :, :, None], voxel_counts, 0)
    return result.reshape(N_DP, N_TILE * N_HELP * slot_count).astype(jnp.int32)


def draw_tokens(key, part):
    values = jax.random.normal(key, (N_DP, SLAB_SLOTS, D), jnp.float32)
    return jnp.clip(values, -6.0, 6.0).astype(jnp.bfloat16)


def draw_w_qkv(key, part):
    weights = jax.random.normal(key, (D, 3 * D), jnp.float32) / math.sqrt(D)
    return jnp.clip(weights, -10.0, 10.0).astype(jnp.bfloat16)


def level_of(own_key, extent, cuts, smallest, top_value):
    def one(dim, blocks):
        steps = jax.random.uniform(jax.random.fold_in(jax.random.fold_in(own_key, 6), dim), (blocks,), jnp.float32, smallest / len(cuts), top_value / len(cuts))
        return jnp.repeat(jnp.exp(steps), extent[dim] // blocks).reshape((-1,) + (1,) * (len(extent) - dim - 1))

    level = one(*cuts[0])
    for cut in cuts[1:]:
        level = level * one(*cut)
    return level


def noise(stream_key, extent, deviation, limit, cuts=(), kind=jnp.bfloat16):
    drawn = deviation * jax.random.normal(stream_key, extent, jnp.float32)
    if cuts:
        drawn = drawn * level_of(stream_key, extent, cuts, -0.22, 0.18)
    return jnp.clip(drawn, -limit, limit).astype(kind)


def setup_inputs(seed: int = 0) -> dict:
    arg_keys = jax.random.split(jax.random.key(seed), 7)
    return {
        "tokens": draw_tokens(jax.random.fold_in(arg_keys[6], 71), 0),
        "d_out": noise(arg_keys[1], (N_DP, SLAB_SLOTS, D), 1.0, 6.0, ((0, 4), (1, 128))),
        "gain": jnp.clip(jax.random.uniform(arg_keys[2], (D,), jnp.float32, 0.5, 1.5), 0.5, 1.5),
        "w_qkv": draw_w_qkv(jax.random.fold_in(arg_keys[6], 71), 0),
        "w_out": noise(arg_keys[4], (D, D), D ** -0.5, 0.375),
        "counts": draw_counts(jax.random.fold_in(arg_keys[6], 71), 0),
    }


def window_grads(window_input, window_upstream, active, gain, w_qkv, w_out):
    features = window_input.shape[-1]
    head_dim = features // HEADS
    factor = 1.0 / math.sqrt(head_dim)
    tokens_f = window_input.astype(jnp.float32)
    center = tokens_f - lax.optimization_barrier(jnp.mean(tokens_f, axis=-1, keepdims=True))
    inverse = lax.rsqrt(lax.optimization_barrier(jnp.mean(center * center, axis=-1, keepdims=True)) + 1e-05)
    normed = center * inverse
    hidden = (normed * gain).astype(jnp.bfloat16)
    projected = jnp.dot(hidden, w_qkv, preferred_element_type=jnp.float32).astype(jnp.bfloat16)
    query_rows = projected[:, :features].reshape(-1, HEADS, head_dim).astype(jnp.float32)
    key_rows = projected[:, features:2 * features].reshape(-1, HEADS, head_dim).astype(jnp.float32)
    value_rows = projected[:, 2 * features:].reshape(-1, HEADS, head_dim).astype(jnp.float32)
    scores = jnp.einsum('qhc,khc->hqk', query_rows, key_rows) * factor
    scores = jnp.where(active[None, None, :], scores, -1e+30)
    highest = lax.optimization_barrier(jnp.max(scores, axis=-1, keepdims=True))
    exponent = jnp.exp(scores - highest)
    probability = exponent / lax.optimization_barrier(jnp.sum(exponent, axis=-1, keepdims=True))
    prob_half = probability.astype(jnp.bfloat16)
    prob_wide = prob_half.astype(jnp.float32)
    attended = jnp.einsum('hqk,khc->qhc', prob_wide, value_rows).astype(jnp.bfloat16).reshape(-1, features)
    grad_attn = jnp.dot(window_upstream, w_out.T, preferred_element_type=jnp.float32).astype(jnp.bfloat16)
    grad_heads = grad_attn.reshape(-1, HEADS, head_dim).astype(jnp.float32)
    grad_prob = jnp.einsum('qhc,khc->hqk', grad_heads, value_rows)
    grad_value = jnp.einsum('hqk,qhc->khc', prob_wide, grad_heads).astype(jnp.bfloat16)
    grad_score = (probability * (grad_prob - lax.optimization_barrier(jnp.sum(probability * grad_prob, axis=-1, keepdims=True))) * factor).astype(jnp.bfloat16)
    score_wide = grad_score.astype(jnp.float32)
    grad_query = jnp.einsum('hqk,khc->qhc', score_wide, key_rows).astype(jnp.bfloat16)
    grad_key = jnp.einsum('hqk,qhc->khc', score_wide, query_rows).astype(jnp.bfloat16)
    grad_proj = jnp.concatenate([grad_query.reshape(-1, features), grad_key.reshape(-1, features), grad_value.reshape(-1, features)], axis=-1)
    grad_hidden = jnp.dot(grad_proj, w_qkv.T, preferred_element_type=jnp.float32)
    part_gain = lax.optimization_barrier(jnp.sum(grad_hidden * normed, axis=0))
    part_qkv = jnp.dot(hidden.T, grad_proj, preferred_element_type=jnp.float32)
    part_out = jnp.dot(attended.T, window_upstream, preferred_element_type=jnp.float32)
    grad_norm = grad_hidden * gain
    grad_input = inverse * (grad_norm - lax.optimization_barrier(jnp.mean(grad_norm, axis=-1, keepdims=True)) - normed * lax.optimization_barrier(jnp.mean(grad_norm * normed, axis=-1, keepdims=True)))
    grad_full = window_upstream.astype(jnp.float32) + grad_input
    grad_rows = jnp.where(active[:, None], grad_full, 0.0).astype(jnp.bfloat16)
    return (grad_rows, part_gain, part_qkv, part_out)

def reference(tokens, d_out, gain, w_qkv, w_out, counts):
    group_size = N_TILE * N_HELP
    slot_count = WKEEP + MOVE
    total_slots = group_size * slot_count
    active_total = group_size * WKEEP
    features = tokens.shape[-1]
    totals = (jnp.zeros((features,), jnp.float32), jnp.zeros((features, 3 * features), jnp.float32), jnp.zeros((features, features), jnp.float32))
    slot_ids = jnp.arange(WIN, dtype=jnp.int32)

    def window_step(carry, block):
        block_input, block_upstream, block_mask = block
        grad_rows, part_gain, part_qkv, part_out = window_grads(block_input, block_upstream, block_mask, gain, w_qkv, w_out)
        return ((carry[0] + part_gain, carry[1] + part_qkv, carry[2] + part_out), grad_rows)
    grad_parts = []
    for replica in range(N_DP):
        window_counts = counts[replica].astype(jnp.int32)
        is_empty = (window_counts == 0).astype(jnp.int32)
        ranking = is_empty * total_slots + jnp.arange(total_slots, dtype=jnp.int32)
        chosen = jnp.argsort(ranking)[:active_total].astype(jnp.int32)
        lengths = window_counts[chosen]
        active = slot_ids[None, :] < lengths[:, None]
        block_in = tokens[replica].reshape(total_slots, WIN, features)[chosen]
        block_up = d_out[replica].reshape(total_slots, WIN, features)[chosen]
        block_in = jnp.where(active[:, :, None], block_in, 0)
        block_up = jnp.where(active[:, :, None], block_up, 0)
        totals, grad_win = lax.scan(window_step, totals, (block_in, block_up, active))
        grad_slab = jnp.zeros((total_slots, WIN, features), jnp.bfloat16).at[chosen].set(grad_win)
        grad_parts.append(grad_slab.reshape(total_slots * WIN, features))
    factor = 1.0 / math.sqrt(N_DP * active_total * WIN)
    return (jnp.stack(grad_parts), totals[1] * factor, totals[2] * factor, totals[0] * factor)
```

```python
import functools
import math

import jax
import jax.numpy as jnp
from jax import lax
from jax.experimental import pallas as pl
from jax.experimental.pallas import tpu as pltpu
from jax.sharding import Mesh
from jax.sharding import PartitionSpec as P

HEADS = 8
WIN = 256
WKEEP = 6
LANES = 128
ROW_STEP = 64
PIECES = 32
PIECE_ROWS = 64
PIECE_PAD = 80


def dot_nn(a, b):
    return jnp.dot(a, b, preferred_element_type=jnp.float32)


def dot_nt(a, b):
    return lax.dot_general(a, b, (((1,), (1,)), ((), ())), preferred_element_type=jnp.float32)


def window_rows(rows, count, x_ref, u_ref, gain, wqkv_ref, wout_ref, qkv_ref, out_ref, gsum_ref, g_ref):
    features = x_ref.shape[-1]
    head_dim = features // HEADS
    per_tile = LANES // head_dim
    factor = 1.0 / math.sqrt(head_dim)
    log_factor = factor * math.log2(math.e)
    half = jnp.bfloat16
    active = lax.broadcasted_iota(jnp.int32, (rows, 1), 0) < count
    tokens = jnp.where(active, x_ref[0, :rows, :].astype(jnp.float32), 0.0)
    upstream = jnp.where(active, u_ref[0, :rows, :].astype(jnp.float32), 0.0)
    upstream_half = upstream.astype(half)
    center = tokens - jnp.mean(tokens, axis=-1, keepdims=True)
    inverse = lax.rsqrt(jnp.mean(center * center, axis=-1, keepdims=True) + 1e-05)
    normed = center * inverse
    hidden = (normed * gain).astype(half)
    queries = dot_nn(hidden, wqkv_ref[:, :features]).astype(half)
    keys = dot_nn(hidden, wqkv_ref[:, features : 2 * features]).astype(half)
    values = dot_nn(hidden, wqkv_ref[:, 2 * features :]).astype(half)
    grad_attn = dot_nt(upstream_half, wout_ref[...]).astype(half)
    hidden_t = hidden.T
    keys_t = keys.T
    values_t = values.T
    lane = lax.broadcasted_iota(jnp.int32, (rows, LANES), 1) // head_dim
    zero = jnp.zeros((), half)

    def masked(array, head):
        tile, place = divmod(head, per_tile)
        block = array[:, tile * LANES : (tile + 1) * LANES]
        return jnp.where(lane == place, block, zero)

    def tile_of(array, head):
        tile = head // per_tile
        return array[:, tile * LANES : (tile + 1) * LANES]

    def products(head):
        scores = dot_nt(masked(keys, head), tile_of(queries, head))
        grad_prob = dot_nt(masked(values, head), tile_of(grad_attn, head))
        return scores, grad_prob

    attended_parts, query_parts = [], []
    key_tiles, value_tiles = [], []
    ready = products(0)
    for head in range(HEADS):
        scores, grad_prob = ready
        if head + 1 < HEADS:
            ready = products(head + 1)
        scores = jnp.where(active, scores, -1e30)
        highest = jnp.max(scores, axis=0, keepdims=True)
        exponent = jnp.exp2((scores - highest) * log_factor)
        probability = exponent * (1.0 / jnp.sum(exponent, axis=0, keepdims=True))
        prob_half = probability.astype(half)
        row_sum = jnp.sum(probability * grad_prob, axis=0, keepdims=True)
        grad_score = (probability * (grad_prob - row_sum) * factor).astype(half)
        span = slice(head * head_dim, (head + 1) * head_dim)
        attended_parts.append(dot_nn(values_t[span, :], prob_half).astype(half))
        query_parts.append(dot_nn(keys_t[span, :], grad_score).astype(half))
        value_part = dot_nn(prob_half, masked(grad_attn, head))
        key_part = dot_nn(grad_score, masked(queries, head))
        if head % per_tile == 0:
            value_tiles.append(value_part)
            key_tiles.append(key_part)
        else:
            value_tiles[-1] = value_tiles[-1] + value_part
            key_tiles[-1] = key_tiles[-1] + key_part
    attended_t = jnp.concatenate(attended_parts, axis=0)
    grad_query = jnp.concatenate(query_parts, axis=0).T
    grad_key = jnp.concatenate(key_tiles, axis=1).astype(half)
    grad_value = jnp.concatenate(value_tiles, axis=1).astype(half)
    grad_proj = jnp.concatenate([grad_query, grad_key, grad_value], axis=1)
    grad_hidden = dot_nt(grad_proj, wqkv_ref[...])
    qkv_ref[...] += dot_nn(hidden_t, grad_proj)
    out_ref[...] += dot_nn(attended_t, upstream_half)
    product = grad_hidden * normed
    gsum_ref[...] += jnp.sum(product, axis=0, keepdims=True)
    grad_norm = grad_hidden * gain
    mean_one = jnp.mean(grad_norm, axis=-1, keepdims=True)
    mean_two = jnp.mean(grad_norm * normed, axis=-1, keepdims=True)
    grad_input = inverse * (grad_norm - mean_one - normed * mean_two)
    g_ref[0, :rows, :] = jnp.where(active, upstream + grad_input, 0.0).astype(half)
    if rows < WIN:
        g_ref[0, rows:, :] = jnp.zeros((WIN - rows, features), half)


def kernel(counts_ref, x_ref, u_ref, gain_ref, wqkv_ref, wout_ref, g_ref, send_ref, qkv_ref, out_ref, gsum_ref):
    step = pl.program_id(0)
    features = x_ref.shape[-1]

    @pl.when(step == 0)
    def _():
        qkv_ref[...] = jnp.zeros_like(qkv_ref)
        out_ref[...] = jnp.zeros_like(out_ref)
        gsum_ref[...] = jnp.zeros_like(gsum_ref)

    count = counts_ref[step]

    @pl.when(count == 0)
    def _():
        g_ref[...] = jnp.zeros_like(g_ref)

    for rows in range(ROW_STEP, WIN + 1, ROW_STEP):
        @pl.when(jnp.logical_and(count > rows - ROW_STEP, count <= rows))
        def _(rows=rows):
            window_rows(
                rows, count, x_ref, u_ref, gain_ref[...], wqkv_ref, wout_ref, qkv_ref, out_ref, gsum_ref, g_ref
            )

    @pl.when(step == pl.num_programs(0) - 1)
    def _():
        extra = PIECE_PAD - PIECE_ROWS
        per_column = features // PIECE_ROWS
        for piece in range(PIECES):
            column, part = divmod(piece, per_column)
            source = qkv_ref if column < 3 * features // LANES else out_ref
            column = column % (3 * features // LANES)
            block = source[
                part * PIECE_ROWS : (part + 1) * PIECE_ROWS, column * LANES : (column + 1) * LANES
            ]
            send_ref[piece, :PIECE_ROWS, :] = block.astype(send_ref.dtype)
            tail = jnp.zeros((extra, LANES), jnp.float32)
            if piece < features // LANES:
                tail = tail + jnp.where(
                    lax.broadcasted_iota(jnp.int32, (extra, LANES), 0) == 0,
                    gsum_ref[:, piece * LANES : (piece + 1) * LANES],
                    0.0,
                )
            send_ref[piece, PIECE_ROWS:, :] = tail.astype(send_ref.dtype)


def local_grads(own_counts, tokens, d_out, gain, w_qkv, w_out):
    slots, features = own_counts.shape[0], gain.shape[-1]

    def window_map(step, counts):
        return (jnp.where(counts[step] > 0, step, 0), 0, 0)

    return pl.pallas_call(
        kernel,
        grid_spec=pltpu.PrefetchScalarGridSpec(
            num_scalar_prefetch=1,
            grid=(slots,),
            in_specs=[
                pl.BlockSpec((1, WIN, features), lambda step, counts: (step, 0, 0)),
                pl.BlockSpec((1, WIN, features), lambda step, counts: (step, 0, 0)),
                pl.BlockSpec((1, features), lambda step, counts: (0, 0)),
                pl.BlockSpec((features, 3 * features), lambda step, counts: (0, 0)),
                pl.BlockSpec((features, features), lambda step, counts: (0, 0)),
            ],
            out_specs=[
                pl.BlockSpec((1, WIN, features), lambda step, counts: (step, 0, 0)),
                pl.BlockSpec((PIECES, PIECE_PAD, LANES), lambda step, counts: (0, 0, 0)),
            ],
            scratch_shapes=[
                pltpu.VMEM((features, 3 * features), jnp.float32),
                pltpu.VMEM((features, features), jnp.float32),
                pltpu.VMEM((1, features), jnp.float32),
            ],
        ),
        out_shape=[
            jax.ShapeDtypeStruct((slots, WIN, features), jnp.bfloat16),
            jax.ShapeDtypeStruct((PIECES, PIECE_PAD, LANES), jnp.bfloat16),
        ],
        compiler_params=pltpu.CompilerParams(
            dimension_semantics=("arbitrary",), vmem_limit_bytes=40 << 20
        ),
        name="window_grads",
    )(own_counts, tokens, d_out, gain, w_qkv, w_out)


def sum_copies(parts, copies, factor):
    def body(in_ref, out_ref):
        total = in_ref[0].astype(jnp.float32)
        for index in range(1, parts.shape[0]):
            total = total + in_ref[index].astype(jnp.float32)
        total = (total * factor).astype(out_ref.dtype)
        for index in range(copies):
            out_ref[index] = total

    return pl.pallas_call(
        body,
        out_shape=jax.ShapeDtypeStruct((copies, *parts.shape[1:]), parts.dtype),
        in_specs=[pl.BlockSpec(memory_space=pltpu.VMEM)],
        out_specs=pl.BlockSpec(memory_space=pltpu.VMEM),
        compiler_params=pltpu.CompilerParams(vmem_limit_bytes=4 << 20),
        name="sum_copies",
    )(parts)


def unpack(whole, features):
    per_column = features // PIECE_ROWS

    def body(in_ref, qkv_ref, out_ref, gain_ref):
        for piece in range(PIECES):
            column, part = divmod(piece, per_column)
            target = qkv_ref if column < 3 * features // LANES else out_ref
            column = column % (3 * features // LANES)
            target[
                part * PIECE_ROWS : (part + 1) * PIECE_ROWS, column * LANES : (column + 1) * LANES
            ] = in_ref[piece, :PIECE_ROWS, :].astype(jnp.float32)
        for piece in range(features // LANES):
            tail = in_ref[piece, PIECE_ROWS:, :].astype(jnp.float32)
            gain_ref[:, piece * LANES : (piece + 1) * LANES] = tail[:1, :]

    return pl.pallas_call(
        body,
        out_shape=[
            jax.ShapeDtypeStruct((features, 3 * features), jnp.float32),
            jax.ShapeDtypeStruct((features, features), jnp.float32),
            jax.ShapeDtypeStruct((1, features), jnp.float32),
        ],
        in_specs=[pl.BlockSpec(memory_space=pltpu.VMEM)],
        out_specs=[pl.BlockSpec(memory_space=pltpu.VMEM)] * 3,
        compiler_params=pltpu.CompilerParams(vmem_limit_bytes=8 << 20),
        name="unpack",
    )(whole)


def in_hbm(array):
    return pltpu.with_memory_space_constraint(array, pltpu.HBM)


def per_device(tokens, d_out, gain, w_qkv, w_out, counts):
    features = tokens.shape[2]
    slot_count = tokens.shape[1] // WIN
    block = ("core", "help", "dp")
    help_index = lax.axis_index("help")
    own_counts = lax.dynamic_slice_in_dim(counts[0], help_index * slot_count, slot_count)
    grad_local, send = local_grads(
        own_counts,
        in_hbm(tokens[0].reshape(slot_count, WIN, features)),
        in_hbm(d_out[0].reshape(slot_count, WIN, features)),
        gain.reshape(1, features),
        w_qkv,
        w_out,
    )
    devices = lax.axis_size("z") * PIECES
    factor = 1.0 / math.sqrt(devices * WKEEP * WIN)
    received = lax.all_to_all(send, block, 0, 0)
    planes = lax.all_to_all(sum_copies(received, lax.axis_size("z"), 1.0), "z", 0, 0)
    whole = lax.all_to_all(sum_copies(planes, PIECES, factor), block, 0, 0)
    grad_qkv, grad_out, grad_gain = unpack(whole, features)
    grad_tokens = grad_local.reshape(1, slot_count * WIN, features)
    return (grad_tokens, grad_qkv, grad_out, grad_gain.reshape(features))


def solution(mesh):
    split = Mesh(
        mesh.devices.reshape(mesh.shape["tile"] // 2, 2, mesh.shape["help"], mesh.shape["dp"]),
        ("z", "core", "help", "dp"),
    )
    tile = ("z", "core")
    in_specs = (
        P("dp", (*tile, "help"), None),
        P("dp", (*tile, "help"), None),
        P(),
        P(),
        P(),
        P("dp", tile),
    )
    out_specs = (P("dp", (*tile, "help"), None), P(), P(), P())
    return jax.shard_map(
        per_device, mesh=split, in_specs=in_specs, out_specs=out_specs, check_vma=False
    )
```

```python
import functools
import math

import jax
import jax.numpy as jnp
from jax import lax
from jax.experimental import pallas as pl
from jax.experimental.pallas import tpu as pltpu
from jax.sharding import Mesh
from jax.sharding import PartitionSpec as P

HEADS = 8
WIN = 256
WKEEP = 6
LANES = 128
ROW_STEP = 64
PIECES = 64
PIECE_ROWS = 32


def dot_nn(a, b):
    return jnp.dot(a, b, preferred_element_type=jnp.float32)


def dot_nt(a, b):
    return lax.dot_general(a, b, (((1,), (1,)), ((), ())), preferred_element_type=jnp.float32)


def window_rows(rows, count, x_ref, u_ref, gain, wqkv_ref, wout_ref, qkv_ref, out_ref, g_ref):
    features = x_ref.shape[-1]
    head_dim = features // HEADS
    per_tile = LANES // head_dim
    factor = 1.0 / math.sqrt(head_dim)
    log_factor = factor * math.log2(math.e)
    half = jnp.bfloat16
    active = lax.broadcasted_iota(jnp.int32, (rows, 1), 0) < count
    tokens = jnp.where(active, x_ref[0, :rows, :].astype(jnp.float32), 0.0)
    upstream = jnp.where(active, u_ref[0, :rows, :].astype(jnp.float32), 0.0)
    upstream_half = upstream.astype(half)
    center = tokens - jnp.mean(tokens, axis=-1, keepdims=True)
    inverse = lax.rsqrt(jnp.mean(center * center, axis=-1, keepdims=True) + 1e-05)
    normed = center * inverse
    hidden = (normed * gain).astype(half)
    queries = dot_nn(hidden, wqkv_ref[:, :features]).astype(half)
    keys = dot_nn(hidden, wqkv_ref[:, features : 2 * features]).astype(half)
    values = dot_nn(hidden, wqkv_ref[:, 2 * features :]).astype(half)
    grad_attn = dot_nt(upstream_half, wout_ref[...]).astype(half)
    hidden_t = hidden.T
    keys_t = keys.T
    values_t = values.T
    lane = lax.broadcasted_iota(jnp.int32, (rows, LANES), 1) // head_dim
    zero = jnp.zeros((), half)

    def masked(array, head):
        tile, place = divmod(head, per_tile)
        block = array[:, tile * LANES : (tile + 1) * LANES]
        return jnp.where(lane == place, block, zero)

    def tile_of(array, head):
        tile = head // per_tile
        return array[:, tile * LANES : (tile + 1) * LANES]

    def products(head):
        scores = dot_nt(masked(keys, head), tile_of(queries, head))
        grad_prob = dot_nt(masked(values, head), tile_of(grad_attn, head))
        return scores, grad_prob

    def gathered(lefts, array, group):
        right = jnp.concatenate([masked(array, head) for head in group], axis=0)
        return dot_nn(jnp.concatenate(lefts, axis=1), right).astype(half)

    attended_parts, query_parts = [], []
    key_tiles, value_tiles = [], []
    probs, scored = [], []
    ready = products(0)
    for head in range(HEADS):
        scores, grad_prob = ready
        if head + 1 < HEADS:
            ready = products(head + 1)
        last = jnp.where(active[-ROW_STEP:], scores[-ROW_STEP:], -1e30)
        scores = jnp.concatenate([scores[:-ROW_STEP], last], axis=0) if rows > ROW_STEP else last
        highest = jnp.max(scores, axis=0, keepdims=True)
        exponent = jnp.exp2((scores - highest) * log_factor)
        probability = exponent * (1.0 / jnp.sum(exponent, axis=0, keepdims=True))
        prob_half = probability.astype(half)
        row_sum = jnp.sum(probability * grad_prob, axis=0, keepdims=True)
        grad_score = (probability * (grad_prob - row_sum) * factor).astype(half)
        span = slice(head * head_dim, (head + 1) * head_dim)
        attended_parts.append(dot_nn(values_t[span, :], prob_half).astype(half))
        query_parts.append(dot_nn(keys_t[span, :], grad_score).astype(half))
        probs.append(prob_half)
        scored.append(grad_score)
        if len(probs) == per_tile:
            group = range(head + 1 - per_tile, head + 1)
            value_tiles.append(gathered(probs, grad_attn, group))
            key_tiles.append(gathered(scored, queries, group))
            probs, scored = [], []
    attended_t = jnp.concatenate(attended_parts, axis=0)
    grad_query = jnp.concatenate(query_parts, axis=0).T
    grad_key = jnp.concatenate(key_tiles, axis=1)
    grad_value = jnp.concatenate(value_tiles, axis=1)
    grad_proj = jnp.concatenate([grad_query, grad_key, grad_value], axis=1)
    grad_hidden = dot_nt(grad_proj, wqkv_ref[...])
    qkv_ref[...] += dot_nn(hidden_t, grad_proj)
    out_ref[...] += dot_nn(attended_t, upstream_half)
    grad_norm = grad_hidden * gain
    mean_one = jnp.mean(grad_norm, axis=-1, keepdims=True)
    mean_two = jnp.mean(grad_norm * normed, axis=-1, keepdims=True)
    grad_input = inverse * (grad_norm - mean_one - normed * mean_two)
    g_ref[0, :rows, :] = jnp.where(active, upstream + grad_input, 0.0).astype(half)
    if rows < WIN:
        g_ref[0, rows:, :] = jnp.zeros((WIN - rows, features), half)


def kernel(counts_ref, x_ref, u_ref, gain_ref, wqkv_ref, wout_ref, g_ref, send_ref, qkv_ref, out_ref):
    step = pl.program_id(0)
    features = x_ref.shape[-1]

    @pl.when(step == 0)
    def _():
        qkv_ref[...] = jnp.zeros_like(qkv_ref)
        out_ref[...] = jnp.zeros_like(out_ref)

    count = counts_ref[0, lax.axis_index("help") * pl.num_programs(0) + step]

    @pl.when(count == 0)
    def _():
        g_ref[...] = jnp.zeros_like(g_ref)

    for rows in range(ROW_STEP, WIN + 1, ROW_STEP):
        @pl.when(jnp.logical_and(count > rows - ROW_STEP, count <= rows))
        def _(rows=rows):
            window_rows(rows, count, x_ref, u_ref, gain_ref[...], wqkv_ref, wout_ref, qkv_ref, out_ref, g_ref)

    @pl.when(step == pl.num_programs(0) - 1)
    def _():
        for piece in range(PIECES):
            source, rows, lanes = place_of(piece, features, qkv_ref, out_ref)
            send_ref[piece] = source[rows, lanes].astype(send_ref.dtype)


def place_of(piece, features, qkv_ref, out_ref):
    column, part = divmod(piece, features // PIECE_ROWS)
    columns = 3 * features // LANES
    lane = column % columns * LANES
    rows = slice(part * PIECE_ROWS, (part + 1) * PIECE_ROWS)
    return (qkv_ref if column < columns else out_ref), rows, slice(lane, lane + LANES)


def local_grads(counts, tokens, d_out, gain, w_qkv, w_out):
    slots, features = tokens.shape[0], gain.shape[-1]
    return pl.pallas_call(
        kernel,
        grid_spec=pltpu.PrefetchScalarGridSpec(
            num_scalar_prefetch=1,
            grid=(slots,),
            in_specs=[
                pl.BlockSpec((1, WIN, features), lambda step, counts: (step, 0, 0)),
                pl.BlockSpec((1, WIN, features), lambda step, counts: (step, 0, 0)),
                pl.BlockSpec((1, features), lambda step, counts: (0, 0)),
                pl.BlockSpec((features, 3 * features), lambda step, counts: (0, 0)),
                pl.BlockSpec((features, features), lambda step, counts: (0, 0)),
            ],
            out_specs=[
                pl.BlockSpec((1, WIN, features), lambda step, counts: (step, 0, 0)),
                pl.BlockSpec((PIECES, PIECE_ROWS, LANES), lambda step, counts: (0, 0, 0)),
            ],
            scratch_shapes=[
                pltpu.VMEM((features, 3 * features), jnp.float32),
                pltpu.VMEM((features, features), jnp.float32),
            ],
        ),
        out_shape=[
            jax.ShapeDtypeStruct((slots, WIN, features), jnp.bfloat16),
            jax.ShapeDtypeStruct((PIECES, PIECE_ROWS, LANES), jnp.bfloat16),
        ],
        compiler_params=pltpu.CompilerParams(
            dimension_semantics=("arbitrary",), vmem_limit_bytes=40 << 20
        ),
        name="window_grads",
    )(counts, tokens, d_out, gain, w_qkv, w_out)


def sum_copies(parts, copies, factor, dtype):
    def body(in_ref, out_ref):
        total = in_ref[0].astype(jnp.float32)
        for index in range(1, parts.shape[0]):
            total = total + in_ref[index].astype(jnp.float32)
        total = (total * factor).astype(dtype)
        for index in range(copies):
            out_ref[index] = total

    return pl.pallas_call(
        body,
        out_shape=jax.ShapeDtypeStruct((copies, *parts.shape[1:]), dtype),
        in_specs=[pl.BlockSpec(memory_space=pltpu.VMEM)],
        out_specs=pl.BlockSpec(memory_space=pltpu.VMEM),
        compiler_params=pltpu.CompilerParams(vmem_limit_bytes=4 << 20),
        name="sum_copies",
    )(parts)


def unpack(whole, w_qkv, gain):
    features = gain.shape[-1]

    def body(in_ref, w_ref, scale_ref, qkv_ref, out_ref, gain_ref):
        for piece in range(PIECES):
            target, rows, lanes = place_of(piece, features, qkv_ref, out_ref)
            target[rows, lanes] = in_ref[piece].astype(jnp.float32)
        total = jnp.zeros((features, LANES), jnp.float32)
        for lane in range(0, 3 * features, LANES):
            lanes = slice(lane, lane + LANES)
            total = total + w_ref[:, lanes].astype(jnp.float32) * qkv_ref[:, lanes]
        gain_ref[...] = jnp.sum(total.T, axis=0, keepdims=True) / scale_ref[...]

    return pl.pallas_call(
        body,
        out_shape=[
            jax.ShapeDtypeStruct((features, 3 * features), jnp.float32),
            jax.ShapeDtypeStruct((features, features), jnp.float32),
            jax.ShapeDtypeStruct((1, features), jnp.float32),
        ],
        in_specs=[pl.BlockSpec(memory_space=pltpu.VMEM)] * 3,
        out_specs=[pl.BlockSpec(memory_space=pltpu.VMEM)] * 3,
        compiler_params=pltpu.CompilerParams(vmem_limit_bytes=8 << 20),
        name="unpack",
    )(whole, w_qkv, gain)


def in_hbm(array):
    return pltpu.with_memory_space_constraint(array, pltpu.HBM)


def per_device(tokens, d_out, gain, w_qkv, w_out, counts):
    features = tokens.shape[2]
    slot_count = tokens.shape[1] // WIN
    block = ("z_lo", "core", "help", "dp")
    gain = gain.reshape(1, features)
    grad_local, send = local_grads(
        counts,
        in_hbm(tokens[0].reshape(slot_count, WIN, features)),
        in_hbm(d_out[0].reshape(slot_count, WIN, features)),
        in_hbm(gain),
        in_hbm(w_qkv),
        in_hbm(w_out),
    )
    planes = lax.axis_size("z_hi")
    factor = 1.0 / math.sqrt(planes * lax.axis_size(block) * WKEEP * WIN)
    received = lax.all_to_all(send, block, 0, 0)
    copies = sum_copies(received, planes, 1.0, jnp.float32)
    copies = sum_copies(lax.all_to_all(copies, "z_hi", 0, 0), PIECES, factor, jnp.bfloat16)
    grad_qkv, grad_out, grad_gain = unpack(lax.all_to_all(copies, block, 0, 0), w_qkv, gain)
    grad_tokens = grad_local.reshape(1, slot_count * WIN, features)
    return (grad_tokens, grad_qkv, grad_out, grad_gain.reshape(features))


def solution(mesh):
    shape = dict(mesh.shape)
    split = Mesh(
        mesh.devices.reshape(shape["tile"] // 4, 2, 2, shape["help"], shape["dp"]),
        ("z_hi", "z_lo", "core", "help", "dp"),
    )
    tile = ("z_hi", "z_lo", "core")
    in_specs = (
        P("dp", (*tile, "help"), None),
        P("dp", (*tile, "help"), None),
        P(),
        P(),
        P(),
        P("dp", tile),
    )
    out_specs = (P("dp", (*tile, "help"), None), P(), P(), P())
    return jax.shard_map(
        per_device, mesh=split, in_specs=in_specs, out_specs=out_specs, check_vma=False
    )
```

```python
import functools
import math

import jax
import jax.numpy as jnp
from jax import lax
from jax.experimental import pallas as pl
from jax.experimental.pallas import tpu as pltpu
from jax.sharding import Mesh
from jax.sharding import PartitionSpec as P

HEADS = 8
WIN = 256
WKEEP = 6
LANES = 128
ROW_STEP = 64
PER_STEP = 2
GROUPS = {64: 8, 128: 4, 192: 1, 256: 2}
PIECES = 64
PIECE_ROWS = 32


def dot_nn(a, b):
    return jnp.dot(a, b, preferred_element_type=jnp.float32)


def dot_nt(a, b):
    return lax.dot_general(a, b, (((1,), (1,)), ((), ())), preferred_element_type=jnp.float32)


def window_rows(rows, place, count, x_ref, u_ref, gain, wqkv_ref, wqkv_t_ref, wout_t_ref, sum_ref, g_ref):
    features = x_ref.shape[-1]
    head_dim = features // HEADS
    factor = 1.0 / math.sqrt(head_dim)
    log_factor = factor * math.log2(math.e)
    half = jnp.bfloat16
    active = lax.broadcasted_iota(jnp.int32, (rows, 1), 0) < count
    tokens = jnp.where(active, x_ref[place, :rows, :].astype(jnp.float32), 0.0)
    upstream = jnp.where(active, u_ref[place, :rows, :].astype(jnp.float32), 0.0)
    upstream_half = upstream.astype(half)
    grad_attn_t = dot_nn(upstream_half, wout_t_ref[...]).astype(half).T
    center = tokens - jnp.mean(tokens, axis=-1, keepdims=True)
    inverse = lax.rsqrt(jnp.mean(center * center, axis=-1, keepdims=True) + 1e-05)
    normed = center * inverse
    hidden = (normed * gain).astype(half)
    queries_t = dot_nn(hidden, wqkv_ref[:, :features]).astype(half).T
    keys = dot_nn(hidden, wqkv_ref[:, features : 2 * features]).astype(half)
    values = dot_nn(hidden, wqkv_ref[:, 2 * features :]).astype(half)
    keys_t = keys.T
    values_t = values.T

    def span(head):
        return slice(head * head_dim, (head + 1) * head_dim)

    size = GROUPS[rows]

    def products(start):
        heads = range(start, start + size)
        scores = [dot_nn(keys[:, span(head)], queries_t[span(head), :]) for head in heads]
        grad_prob = [dot_nn(values[:, span(head)], grad_attn_t[span(head), :]) for head in heads]
        return jnp.concatenate(scores, axis=1), jnp.concatenate(grad_prob, axis=1)

    attended, grad_query, grad_key, grad_value = [], [], [], []
    ready = products(0)
    for start in range(0, HEADS, size):
        scores, grad_prob = ready
        if start + size < HEADS:
            ready = products(start + size)
        last = jnp.where(active[-ROW_STEP:], scores[-ROW_STEP:], -1e30)
        scores = jnp.concatenate([scores[:-ROW_STEP], last], axis=0) if rows > ROW_STEP else last
        highest = jnp.max(scores, axis=0, keepdims=True)
        exponent = jnp.exp2((scores - highest) * log_factor)
        probability = exponent * (1.0 / jnp.sum(exponent, axis=0, keepdims=True))
        prob_group = probability.astype(half)
        row_sum = jnp.sum(probability * grad_prob, axis=0, keepdims=True)
        score_group = (probability * (grad_prob - row_sum) * factor).astype(half)
        for index in range(size):
            head = start + index
            prob_half = prob_group[:, index * rows : (index + 1) * rows]
            grad_score = score_group[:, index * rows : (index + 1) * rows]
            attended.append(dot_nn(values_t[span(head), :], prob_half).astype(half))
            grad_value.append(dot_nt(grad_attn_t[span(head), :], prob_half).astype(half))
            grad_query.append(dot_nn(keys_t[span(head), :], grad_score).astype(half))
            grad_key.append(dot_nt(queries_t[span(head), :], grad_score).astype(half))
    grad_proj_t = jnp.concatenate([*grad_query, *grad_key, *grad_value], axis=0)
    grad_hidden = dot_nn(grad_proj_t.T, wqkv_t_ref[...])
    sum_ref[: 3 * features, :] += dot_nn(grad_proj_t, hidden)
    sum_ref[3 * features :, :] += dot_nn(jnp.concatenate(attended, axis=0), upstream_half)
    grad_norm = grad_hidden * gain
    mean_one = jnp.mean(grad_norm, axis=-1, keepdims=True)
    mean_two = jnp.mean(grad_norm * normed, axis=-1, keepdims=True)
    grad_input = inverse * (grad_norm - mean_one - normed * mean_two)
    g_ref[place, :rows, :] = jnp.where(active, upstream + grad_input, 0.0).astype(half)
    if rows < WIN:
        g_ref[place, rows:, :] = jnp.zeros((WIN - rows, features), half)


def kernel(counts_ref, x_ref, u_ref, gain_ref, wqkv_ref, wout_ref, g_ref, send_ref, sum_ref, wqkv_t_ref, wout_t_ref):
    step = pl.program_id(0)

    @pl.when(step == 0)
    def _():
        sum_ref[...] = jnp.zeros_like(sum_ref)
        wout_t_ref[...] = wout_ref[...].T
        wqkv_t_ref[...] = wqkv_ref[...].T

    slots = pl.num_programs(0) * PER_STEP
    first = lax.axis_index("help") * slots + step * PER_STEP

    def window_step(place, carry):
        count = counts_ref[0, first + place]

        @pl.when(count == 0)
        def _():
            g_ref[place] = jnp.zeros(g_ref.shape[1:], g_ref.dtype)

        for rows in range(ROW_STEP, WIN + 1, ROW_STEP):
            @pl.when(jnp.logical_and(count > rows - ROW_STEP, count <= rows))
            def _(rows=rows):
                window_rows(
                    rows,
                    place,
                    count,
                    x_ref,
                    u_ref,
                    gain_ref[...],
                    wqkv_ref,
                    wqkv_t_ref,
                    wout_t_ref,
                    sum_ref,
                    g_ref,
                )

        return carry

    lax.fori_loop(0, PER_STEP, window_step, 0)

    @pl.when(step == pl.num_programs(0) - 1)
    def _():
        for piece in range(PIECES):
            rows, lanes = place_of(piece)
            send_ref[piece] = sum_ref[rows, lanes].astype(send_ref.dtype)


def place_of(piece):
    part, lane = divmod(piece, WIN // LANES)
    return slice(part * PIECE_ROWS, (part + 1) * PIECE_ROWS), slice(lane * LANES, (lane + 1) * LANES)


def local_grads(counts, tokens, d_out, gain, w_qkv, w_out):
    slots, features = tokens.shape[0], gain.shape[-1]
    return pl.pallas_call(
        kernel,
        grid_spec=pltpu.PrefetchScalarGridSpec(
            num_scalar_prefetch=1,
            grid=(slots // PER_STEP,),
            in_specs=[
                pl.BlockSpec((PER_STEP, WIN, features), lambda step, counts: (step, 0, 0)),
                pl.BlockSpec((PER_STEP, WIN, features), lambda step, counts: (step, 0, 0)),
                pl.BlockSpec((1, features), lambda step, counts: (0, 0)),
                pl.BlockSpec((features, 3 * features), lambda step, counts: (0, 0)),
                pl.BlockSpec((features, features), lambda step, counts: (0, 0)),
            ],
            out_specs=[
                pl.BlockSpec((PER_STEP, WIN, features), lambda step, counts: (step, 0, 0)),
                pl.BlockSpec(memory_space=pltpu.VMEM),
            ],
            scratch_shapes=[
                pltpu.VMEM((4 * features, features), jnp.float32),
                pltpu.VMEM((3 * features, features), jnp.bfloat16),
                pltpu.VMEM((features, features), jnp.bfloat16),
            ],
        ),
        out_shape=[
            jax.ShapeDtypeStruct((slots, WIN, features), jnp.bfloat16),
            jax.ShapeDtypeStruct((PIECES, PIECE_ROWS, LANES), jnp.bfloat16),
        ],
        compiler_params=pltpu.CompilerParams(
            dimension_semantics=("arbitrary",), vmem_limit_bytes=40 << 20
        ),
        name="window_grads",
    )(counts, tokens, d_out, gain, w_qkv, w_out)


def sum_copies(parts, copies, factor, dtype):
    def body(in_ref, out_ref):
        total = in_ref[0].astype(jnp.float32)
        for index in range(1, parts.shape[0]):
            total = total + in_ref[index].astype(jnp.float32)
        total = (total * factor).astype(dtype)
        for index in range(copies):
            out_ref[index] = total

    return pl.pallas_call(
        body,
        out_shape=jax.ShapeDtypeStruct((copies, *parts.shape[1:]), dtype),
        in_specs=[pl.BlockSpec(memory_space=pltpu.VMEM)],
        out_specs=pl.BlockSpec(memory_space=pltpu.VMEM),
        compiler_params=pltpu.CompilerParams(vmem_limit_bytes=4 << 20),
        name="sum_copies",
    )(parts)


def unpack(whole, w_qkv, gain):
    features = gain.shape[-1]

    def body(in_ref, w_ref, scale_ref, qkv_ref, out_ref, gain_ref, turned_ref):
        for piece in range(PIECES):
            rows, lanes = place_of(piece)
            if rows.start < 3 * features:
                turned_ref[rows, lanes] = in_ref[piece]
            else:
                out_ref[rows.start - 3 * features : rows.stop - 3 * features, lanes] = in_ref[piece].astype(jnp.float32)
        for block in range(3):
            columns = slice(block * features, (block + 1) * features)
            qkv_ref[:, columns] = turned_ref[columns, :].T.astype(jnp.float32)
        total = jnp.zeros((features, LANES), jnp.float32)
        for lane in range(0, 3 * features, LANES):
            lanes = slice(lane, lane + LANES)
            total = total + w_ref[:, lanes].astype(jnp.float32) * qkv_ref[:, lanes]
        gain_ref[...] = jnp.sum(total.T, axis=0, keepdims=True) / scale_ref[...]

    return pl.pallas_call(
        body,
        out_shape=[
            jax.ShapeDtypeStruct((features, 3 * features), jnp.float32),
            jax.ShapeDtypeStruct((features, features), jnp.float32),
            jax.ShapeDtypeStruct((1, features), jnp.float32),
        ],
        in_specs=[pl.BlockSpec(memory_space=pltpu.VMEM)] * 3,
        out_specs=[pl.BlockSpec(memory_space=pltpu.VMEM)] * 3,
        scratch_shapes=[pltpu.VMEM((3 * features, features), jnp.bfloat16)],
        compiler_params=pltpu.CompilerParams(vmem_limit_bytes=8 << 20),
        name="unpack",
    )(whole, w_qkv, gain)


def in_hbm(array):
    return pltpu.with_memory_space_constraint(array, pltpu.HBM)


def per_device(tokens, d_out, gain, w_qkv, w_out, counts):
    features = tokens.shape[2]
    slot_count = tokens.shape[1] // WIN
    block = ("z_lo", "core", "help", "dp")
    gain = gain.reshape(1, features)
    grad_local, send = local_grads(
        in_hbm(counts),
        in_hbm(tokens[0].reshape(slot_count, WIN, features)),
        in_hbm(d_out[0].reshape(slot_count, WIN, features)),
        in_hbm(gain),
        in_hbm(w_qkv),
        in_hbm(w_out),
    )
    planes = lax.axis_size("z_hi")
    factor = 1.0 / math.sqrt(planes * lax.axis_size(block) * WKEEP * WIN)
    received = lax.all_to_all(send, block, 0, 0)
    copies = sum_copies(received, planes, 1.0, jnp.float32)
    copies = sum_copies(lax.all_to_all(copies, "z_hi", 0, 0), PIECES, factor, jnp.bfloat16)
    grad_qkv, grad_out, grad_gain = unpack(lax.all_to_all(copies, block, 0, 0), w_qkv, gain)
    grad_tokens = grad_local.reshape(1, slot_count * WIN, features)
    return (grad_tokens, grad_qkv, grad_out, grad_gain.reshape(features))


def solution(mesh):
    shape = dict(mesh.shape)
    split = Mesh(
        mesh.devices.reshape(shape["tile"] // 4, 2, 2, shape["help"], shape["dp"]),
        ("z_hi", "z_lo", "core", "help", "dp"),
    )
    tile = ("z_hi", "z_lo", "core")
    in_specs = (
        P("dp", (*tile, "help"), None),
        P("dp", (*tile, "help"), None),
        P(),
        P(),
        P(),
        P("dp", tile),
    )
    out_specs = (P("dp", (*tile, "help"), None), P(), P(), P())
    return jax.shard_map(
        per_device, mesh=split, in_specs=in_specs, out_specs=out_specs, check_vma=False
    )
```

```python
import functools
import math

import jax
import jax.numpy as jnp
from jax import lax
from jax.experimental import pallas as pl
from jax.experimental.pallas import tpu as pltpu
from jax.sharding import Mesh
from jax.sharding import PartitionSpec as P

HEADS = 8
WIN = 256
WKEEP = 6
LANES = 128
ROW_STEP = 64
PER_STEP = 2
GROUPS = {64: 8, 128: 4, 192: 1, 256: 1}
ORDER = {64: (1, 0), 128: (1, 0), 192: (2, 1), 256: (2, 1)}
PIECES = 64
PIECE_ROWS = 32


def dot_nn(a, b):
    return jnp.dot(a, b, preferred_element_type=jnp.float32)


def dot_nt(a, b):
    return lax.dot_general(a, b, (((1,), (1,)), ((), ())), preferred_element_type=jnp.float32)


def window_rows(rows, place, count, x_ref, u_ref, gain, wqkv_ref, wqkv_t_ref, wout_t_ref, sum_ref, g_ref):
    features = x_ref.shape[-1]
    head_dim = features // HEADS
    factor = 1.0 / math.sqrt(head_dim)
    log_factor = factor * math.log2(math.e)
    half = jnp.bfloat16
    active = lax.broadcasted_iota(jnp.int32, (rows, 1), 0) < count
    tokens = jnp.where(active, x_ref[place, :rows, :].astype(jnp.float32), 0.0)
    upstream = jnp.where(active, u_ref[place, :rows, :].astype(jnp.float32), 0.0)
    upstream_half = upstream.astype(half)
    grad_attn_t = dot_nn(upstream_half, wout_t_ref[...]).astype(half).T
    center = tokens - jnp.mean(tokens, axis=-1, keepdims=True)
    inverse = lax.rsqrt(jnp.mean(center * center, axis=-1, keepdims=True) + 1e-05)
    normed = center * inverse
    hidden = (normed * gain).astype(half)
    queries_t = dot_nn(hidden, wqkv_ref[:, :features]).astype(half).T
    keys = dot_nn(hidden, wqkv_ref[:, features : 2 * features]).astype(half)
    values = dot_nn(hidden, wqkv_ref[:, 2 * features :]).astype(half)
    keys_t = keys.T
    values_t = values.T

    def span(head):
        return slice(head * head_dim, (head + 1) * head_dim)

    size = GROUPS[rows]

    def products(start):
        heads = range(start, start + size)
        scores = [dot_nn(keys[:, span(head)], queries_t[span(head), :]) for head in heads]
        grad_prob = [dot_nn(values[:, span(head)], grad_attn_t[span(head), :]) for head in heads]
        return jnp.concatenate(scores, axis=1), jnp.concatenate(grad_prob, axis=1)

    def soften(scores, grad_prob):
        last = jnp.where(active[-ROW_STEP:], scores[-ROW_STEP:], -1e30)
        scores = jnp.concatenate([scores[:-ROW_STEP], last], axis=0) if rows > ROW_STEP else last
        highest = jnp.max(scores, axis=0, keepdims=True)
        exponent = jnp.exp2((scores - highest) * log_factor)
        probability = exponent * (1.0 / jnp.sum(exponent, axis=0, keepdims=True))
        row_sum = jnp.sum(probability * grad_prob, axis=0, keepdims=True)
        grad_score = probability * (grad_prob - row_sum) * factor
        return probability.astype(half), grad_score.astype(half)

    attended, grad_query, grad_key, grad_value = [], [], [], []

    def outputs(start, prob_group, score_group):
        for index in range(size):
            head = start + index
            prob_half = prob_group[:, index * rows : (index + 1) * rows]
            grad_score = score_group[:, index * rows : (index + 1) * rows]
            attended.append(dot_nn(values_t[span(head), :], prob_half).astype(half))
            grad_value.append(dot_nt(grad_attn_t[span(head), :], prob_half).astype(half))
            grad_query.append(dot_nn(keys_t[span(head), :], grad_score).astype(half))
            grad_key.append(dot_nt(queries_t[span(head), :], grad_score).astype(half))

    look, delay = ORDER[rows]
    starts = list(range(0, HEADS, size))
    ready = [products(start) for start in starts[:look]]
    waiting = []
    for place_in, start in enumerate(starts):
        if place_in + look < len(starts):
            ready.append(products(starts[place_in + look]))
        waiting.append((start, *soften(*ready.pop(0))))
        if len(waiting) > delay:
            outputs(*waiting.pop(0))
    for entry in waiting:
        outputs(*entry)
    grad_proj_t = jnp.concatenate([*grad_query, *grad_key, *grad_value], axis=0)
    grad_hidden = dot_nn(grad_proj_t.T, wqkv_t_ref[...])
    sum_ref[: 3 * features, :] += dot_nn(grad_proj_t, hidden)
    sum_ref[3 * features :, :] += dot_nn(jnp.concatenate(attended, axis=0), upstream_half)
    grad_norm = grad_hidden * gain
    mean_one = jnp.mean(grad_norm, axis=-1, keepdims=True)
    mean_two = jnp.mean(grad_norm * normed, axis=-1, keepdims=True)
    grad_input = inverse * (grad_norm - mean_one - normed * mean_two)
    g_ref[place, :rows, :] = jnp.where(active, upstream + grad_input, 0.0).astype(half)
    if rows < WIN:
        g_ref[place, rows:, :] = jnp.zeros((WIN - rows, features), half)


def kernel(counts_ref, x_ref, u_ref, gain_ref, wqkv_ref, wout_ref, g_ref, send_ref, sum_ref, wqkv_t_ref, wout_t_ref):
    step = pl.program_id(0)

    @pl.when(step == 0)
    def _():
        sum_ref[...] = jnp.zeros_like(sum_ref)
        wout_t_ref[...] = wout_ref[...].T
        wqkv_t_ref[...] = wqkv_ref[...].T

    slots = pl.num_programs(0) * PER_STEP
    first = lax.axis_index("help") * slots + step * PER_STEP

    def window_step(place, carry):
        count = counts_ref[0, first + place]

        @pl.when(count == 0)
        def _():
            g_ref[place] = jnp.zeros(g_ref.shape[1:], g_ref.dtype)

        for rows in range(ROW_STEP, WIN + 1, ROW_STEP):
            @pl.when(jnp.logical_and(count > rows - ROW_STEP, count <= rows))
            def _(rows=rows):
                window_rows(
                    rows,
                    place,
                    count,
                    x_ref,
                    u_ref,
                    gain_ref[...],
                    wqkv_ref,
                    wqkv_t_ref,
                    wout_t_ref,
                    sum_ref,
                    g_ref,
                )

        return carry

    lax.fori_loop(0, PER_STEP, window_step, 0)

    @pl.when(step == pl.num_programs(0) - 1)
    def _():
        for piece in range(PIECES):
            rows, lanes = place_of(piece)
            send_ref[piece] = sum_ref[rows, lanes].astype(send_ref.dtype)


def place_of(piece):
    part, lane = divmod(piece, WIN // LANES)
    return slice(part * PIECE_ROWS, (part + 1) * PIECE_ROWS), slice(lane * LANES, (lane + 1) * LANES)


def local_grads(counts, tokens, d_out, gain, w_qkv, w_out):
    slots, features = tokens.shape[0], gain.shape[-1]
    return pl.pallas_call(
        kernel,
        grid_spec=pltpu.PrefetchScalarGridSpec(
            num_scalar_prefetch=1,
            grid=(slots // PER_STEP,),
            in_specs=[
                pl.BlockSpec((PER_STEP, WIN, features), lambda step, counts: (step, 0, 0)),
                pl.BlockSpec((PER_STEP, WIN, features), lambda step, counts: (step, 0, 0)),
                pl.BlockSpec((1, features), lambda step, counts: (0, 0)),
                pl.BlockSpec((features, 3 * features), lambda step, counts: (0, 0)),
                pl.BlockSpec((features, features), lambda step, counts: (0, 0)),
            ],
            out_specs=[
                pl.BlockSpec((PER_STEP, WIN, features), lambda step, counts: (step, 0, 0)),
                pl.BlockSpec(memory_space=pltpu.VMEM),
            ],
            scratch_shapes=[
                pltpu.VMEM((4 * features, features), jnp.float32),
                pltpu.VMEM((3 * features, features), jnp.bfloat16),
                pltpu.VMEM((features, features), jnp.bfloat16),
            ],
        ),
        out_shape=[
            jax.ShapeDtypeStruct((slots, WIN, features), jnp.bfloat16),
            jax.ShapeDtypeStruct((PIECES, PIECE_ROWS, LANES), jnp.bfloat16),
        ],
        compiler_params=pltpu.CompilerParams(
            dimension_semantics=("arbitrary",), vmem_limit_bytes=40 << 20
        ),
        name="window_grads",
    )(counts, tokens, d_out, gain, w_qkv, w_out)


def sum_copies(parts, copies, factor, dtype):
    def body(in_ref, out_ref):
        total = in_ref[0].astype(jnp.float32)
        for index in range(1, parts.shape[0]):
            total = total + in_ref[index].astype(jnp.float32)
        total = (total * factor).astype(dtype)
        for index in range(copies):
            out_ref[index] = total

    return pl.pallas_call(
        body,
        out_shape=jax.ShapeDtypeStruct((copies, *parts.shape[1:]), dtype),
        in_specs=[pl.BlockSpec(memory_space=pltpu.VMEM)],
        out_specs=pl.BlockSpec(memory_space=pltpu.VMEM),
        compiler_params=pltpu.CompilerParams(vmem_limit_bytes=4 << 20),
        name="sum_copies",
    )(parts)


def unpack(whole, w_qkv, gain):
    features = gain.shape[-1]

    def body(in_ref, w_ref, scale_ref, qkv_ref, out_ref, gain_ref, turned_ref):
        for piece in range(PIECES):
            rows, lanes = place_of(piece)
            if rows.start < 3 * features:
                turned_ref[rows, lanes] = in_ref[piece]
            else:
                out_ref[rows.start - 3 * features : rows.stop - 3 * features, lanes] = in_ref[piece].astype(jnp.float32)
        for block in range(3):
            columns = slice(block * features, (block + 1) * features)
            qkv_ref[:, columns] = turned_ref[columns, :].T.astype(jnp.float32)
        total = jnp.zeros((features, LANES), jnp.float32)
        for lane in range(0, 3 * features, LANES):
            lanes = slice(lane, lane + LANES)
            total = total + w_ref[:, lanes].astype(jnp.float32) * qkv_ref[:, lanes]
        gain_ref[...] = jnp.sum(total.T, axis=0, keepdims=True) / scale_ref[...]

    return pl.pallas_call(
        body,
        out_shape=[
            jax.ShapeDtypeStruct((features, 3 * features), jnp.float32),
            jax.ShapeDtypeStruct((features, features), jnp.float32),
            jax.ShapeDtypeStruct((1, features), jnp.float32),
        ],
        in_specs=[pl.BlockSpec(memory_space=pltpu.VMEM)] * 3,
        out_specs=[pl.BlockSpec(memory_space=pltpu.VMEM)] * 3,
        scratch_shapes=[pltpu.VMEM((3 * features, features), jnp.bfloat16)],
        compiler_params=pltpu.CompilerParams(vmem_limit_bytes=8 << 20),
        name="unpack",
    )(whole, w_qkv, gain)


def in_hbm(array):
    return pltpu.with_memory_space_constraint(array, pltpu.HBM)


def per_device(tokens, d_out, gain, w_qkv, w_out, counts):
    features = tokens.shape[2]
    slot_count = tokens.shape[1] // WIN
    block = ("z_lo", "core", "help", "dp")
    gain = gain.reshape(1, features)
    grad_local, send = local_grads(
        in_hbm(counts),
        in_hbm(tokens[0].reshape(slot_count, WIN, features)),
        in_hbm(d_out[0].reshape(slot_count, WIN, features)),
        in_hbm(gain),
        in_hbm(w_qkv),
        in_hbm(w_out),
    )
    planes = lax.axis_size("z_hi")
    factor = 1.0 / math.sqrt(planes * lax.axis_size(block) * WKEEP * WIN)
    received = lax.all_to_all(send, block, 0, 0)
    copies = sum_copies(received, planes, 1.0, jnp.float32)
    copies = sum_copies(lax.all_to_all(copies, "z_hi", 0, 0), PIECES, factor, jnp.bfloat16)
    grad_qkv, grad_out, grad_gain = unpack(lax.all_to_all(copies, block, 0, 0), w_qkv, gain)
    grad_tokens = grad_local.reshape(1, slot_count * WIN, features)
    return (grad_tokens, grad_qkv, grad_out, grad_gain.reshape(features))


def solution(mesh):
    shape = dict(mesh.shape)
    split = Mesh(
        mesh.devices.reshape(shape["tile"] // 4, 2, 2, shape["help"], shape["dp"]),
        ("z_hi", "z_lo", "core", "help", "dp"),
    )
    tile = ("z_hi", "z_lo", "core")
    in_specs = (
        P("dp", (*tile, "help"), None),
        P("dp", (*tile, "help"), None),
        P(),
        P(),
        P(),
        P("dp", tile),
    )
    out_specs = (P("dp", (*tile, "help"), None), P(), P(), P())
    return jax.shard_map(
        per_device, mesh=split, in_specs=in_specs, out_specs=out_specs, check_vma=False
    )
```

```python
import functools
import math

import jax
import jax.numpy as jnp
from jax import lax
from jax.experimental import pallas as pl
from jax.experimental.pallas import tpu as pltpu
from jax.sharding import Mesh
from jax.sharding import PartitionSpec as P

HEADS = 8
WIN = 256
WKEEP = 6
LANES = 128
ROW_STEP = 64
PER_STEP = 2
GROUPS = {64: 8, 128: 4, 192: 1, 256: 1}
ORDER = {64: (1, 0), 128: (1, 0), 192: (2, 1), 256: (2, 1)}
PIECES = 64
PIECE_ROWS = 32


def dot_nn(a, b):
    return jnp.dot(a, b, preferred_element_type=jnp.float32)


def dot_nt(a, b):
    return lax.dot_general(a, b, (((1,), (1,)), ((), ())), preferred_element_type=jnp.float32)


def window_rows(rows, place, count, x_ref, u_ref, gain, wqkv_ref, wqkv_t_ref, wout_t_ref, sum_ref, g_ref):
    features = x_ref.shape[-1]
    head_dim = features // HEADS
    factor = 1.0 / math.sqrt(head_dim)
    log_factor = factor * math.log2(math.e)
    half = jnp.bfloat16
    active = lax.broadcasted_iota(jnp.int32, (rows, 1), 0) < count
    tokens = jnp.where(active, x_ref[place, :rows, :].astype(jnp.float32), 0.0)
    upstream = jnp.where(active, u_ref[place, :rows, :].astype(jnp.float32), 0.0)
    upstream_half = upstream.astype(half)
    grad_attn_t = dot_nn(upstream_half, wout_t_ref[...]).astype(half).T
    center = tokens - jnp.mean(tokens, axis=-1, keepdims=True)
    inverse = lax.rsqrt(jnp.mean(center * center, axis=-1, keepdims=True) + 1e-05)
    normed = center * inverse
    hidden = (normed * gain).astype(half)
    queries_t = dot_nn(hidden, wqkv_ref[:, :features]).astype(half).T
    keys = dot_nn(hidden, wqkv_ref[:, features : 2 * features]).astype(half)
    values = dot_nn(hidden, wqkv_ref[:, 2 * features :]).astype(half)
    keys_t = keys.T
    values_t = values.T

    def span(head):
        return slice(head * head_dim, (head + 1) * head_dim)

    size = GROUPS[rows]

    def products(start):
        heads = range(start, start + size)
        scores = [dot_nn(keys[:, span(head)], queries_t[span(head), :]) for head in heads]
        grad_prob = [dot_nn(values[:, span(head)], grad_attn_t[span(head), :]) for head in heads]
        return jnp.concatenate(scores, axis=1), jnp.concatenate(grad_prob, axis=1)

    def soften(scores, grad_prob):
        last = jnp.where(active[-ROW_STEP:], scores[-ROW_STEP:], -1e30)
        scores = jnp.concatenate([scores[:-ROW_STEP], last], axis=0) if rows > ROW_STEP else last
        highest = jnp.max(scores, axis=0, keepdims=True)
        exponent = jnp.exp2((scores - highest) * log_factor)
        probability = exponent * (1.0 / jnp.sum(exponent, axis=0, keepdims=True))
        row_sum = jnp.sum(probability * grad_prob, axis=0, keepdims=True)
        grad_score = probability * (grad_prob - row_sum) * factor
        return probability.astype(half), grad_score.astype(half)

    attended, grad_query, grad_key, grad_value = [], [], [], []

    def outputs(start, prob_group, score_group):
        for index in range(size):
            head = start + index
            prob_half = prob_group[:, index * rows : (index + 1) * rows]
            grad_score = score_group[:, index * rows : (index + 1) * rows]
            attended.append(dot_nn(values_t[span(head), :], prob_half).astype(half))
            grad_value.append(dot_nt(grad_attn_t[span(head), :], prob_half).astype(half))
            grad_query.append(dot_nn(keys_t[span(head), :], grad_score).astype(half))
            grad_key.append(dot_nt(queries_t[span(head), :], grad_score).astype(half))

    look, delay = ORDER[rows]
    starts = list(range(0, HEADS, size))
    ready = [products(start) for start in starts[:look]]
    waiting = []
    for place_in, start in enumerate(starts):
        if place_in + look < len(starts):
            ready.append(products(starts[place_in + look]))
        waiting.append((start, *soften(*ready.pop(0))))
        if len(waiting) > delay:
            outputs(*waiting.pop(0))
    for entry in waiting:
        outputs(*entry)
    grad_proj_t = jnp.concatenate([*grad_query, *grad_key, *grad_value], axis=0)
    grad_hidden = dot_nn(grad_proj_t.T, wqkv_t_ref[...])
    sum_ref[: 3 * features, :] += dot_nn(grad_proj_t, hidden)
    sum_ref[3 * features :, :] += dot_nn(jnp.concatenate(attended, axis=0), upstream_half)
    grad_norm = grad_hidden * gain
    mean_one = jnp.mean(grad_norm, axis=-1, keepdims=True)
    mean_two = jnp.mean(grad_norm * normed, axis=-1, keepdims=True)
    grad_input = inverse * (grad_norm - mean_one - normed * mean_two)
    g_ref[place, :rows, :] = jnp.where(active, upstream + grad_input, 0.0).astype(half)
    if rows < WIN:
        g_ref[place, rows:, :] = jnp.zeros((WIN - rows, features), half)


def kernel(counts_ref, x_ref, u_ref, gain_ref, wqkv_ref, wout_ref, g_ref, send_ref, sum_ref, wqkv_t_ref, wout_t_ref):
    step = pl.program_id(0)

    @pl.when(step == 0)
    def _():
        sum_ref[...] = jnp.zeros_like(sum_ref)
        wout_t_ref[...] = wout_ref[...].T
        wqkv_t_ref[...] = wqkv_ref[...].T

    slots = pl.num_programs(0) * PER_STEP
    first = lax.axis_index("help") * slots + step * PER_STEP

    def window_step(place, carry):
        count = counts_ref[0, first + place]

        @pl.when(count == 0)
        def _():
            g_ref[place] = jnp.zeros(g_ref.shape[1:], g_ref.dtype)

        for rows in range(ROW_STEP, WIN + 1, ROW_STEP):
            @pl.when(jnp.logical_and(count > rows - ROW_STEP, count <= rows))
            def _(rows=rows):
                window_rows(
                    rows,
                    place,
                    count,
                    x_ref,
                    u_ref,
                    gain_ref[...],
                    wqkv_ref,
                    wqkv_t_ref,
                    wout_t_ref,
                    sum_ref,
                    g_ref,
                )

        return carry

    lax.fori_loop(0, PER_STEP, window_step, 0)

    @pl.when(step == pl.num_programs(0) - 1)
    def _():
        for piece in range(PIECES):
            rows, lanes = place_of(piece)
            send_ref[piece] = sum_ref[rows, lanes].astype(send_ref.dtype)


def place_of(piece):
    part, lane = divmod(piece, WIN // LANES)
    return slice(part * PIECE_ROWS, (part + 1) * PIECE_ROWS), slice(lane * LANES, (lane + 1) * LANES)


def local_grads(counts, tokens, d_out, gain, w_qkv, w_out):
    slots, features = tokens.shape[0], gain.shape[-1]
    return pl.pallas_call(
        kernel,
        grid_spec=pltpu.PrefetchScalarGridSpec(
            num_scalar_prefetch=1,
            grid=(slots // PER_STEP,),
            in_specs=[
                pl.BlockSpec((PER_STEP, WIN, features), lambda step, counts: (step, 0, 0)),
                pl.BlockSpec((PER_STEP, WIN, features), lambda step, counts: (step, 0, 0)),
                pl.BlockSpec((1, features), lambda step, counts: (0, 0)),
                pl.BlockSpec((features, 3 * features), lambda step, counts: (0, 0)),
                pl.BlockSpec((features, features), lambda step, counts: (0, 0)),
            ],
            out_specs=[
                pl.BlockSpec((PER_STEP, WIN, features), lambda step, counts: (step, 0, 0)),
                pl.BlockSpec(memory_space=pltpu.VMEM),
            ],
            scratch_shapes=[
                pltpu.VMEM((4 * features, features), jnp.float32),
                pltpu.VMEM((3 * features, features), jnp.bfloat16),
                pltpu.VMEM((features, features), jnp.bfloat16),
            ],
        ),
        out_shape=[
            jax.ShapeDtypeStruct((slots, WIN, features), jnp.bfloat16),
            jax.ShapeDtypeStruct((PIECES, PIECE_ROWS, LANES), jnp.bfloat16),
        ],
        compiler_params=pltpu.CompilerParams(
            dimension_semantics=("arbitrary",), vmem_limit_bytes=40 << 20
        ),
        name="window_grads",
    )(counts, tokens, d_out, gain, w_qkv, w_out)


def sum_copies(parts, copies, factor, dtype):
    def body(in_ref, out_ref):
        total = in_ref[0].astype(jnp.float32)
        for index in range(1, parts.shape[0]):
            total = total + in_ref[index].astype(jnp.float32)
        total = (total * factor).astype(dtype)
        for index in range(copies):
            out_ref[index] = total

    return pl.pallas_call(
        body,
        out_shape=jax.ShapeDtypeStruct((copies, *parts.shape[1:]), dtype),
        in_specs=[pl.BlockSpec(memory_space=pltpu.VMEM)],
        out_specs=pl.BlockSpec(memory_space=pltpu.VMEM),
        compiler_params=pltpu.CompilerParams(vmem_limit_bytes=4 << 20),
        name="sum_copies",
    )(parts)


def unpack(whole, w_qkv, gain):
    features = gain.shape[-1]

    def body(in_ref, w_ref, scale_ref, qkv_ref, out_ref, gain_ref, turned_ref):
        for piece in range(PIECES):
            rows, lanes = place_of(piece)
            if rows.start < 3 * features:
                turned_ref[rows, lanes] = in_ref[piece]
            else:
                out_ref[rows.start - 3 * features : rows.stop - 3 * features, lanes] = in_ref[piece].astype(jnp.float32)
        for block in range(3):
            columns = slice(block * features, (block + 1) * features)
            qkv_ref[:, columns] = turned_ref[columns, :].T.astype(jnp.float32)
        total = jnp.zeros((features, LANES), jnp.float32)
        for lane in range(0, 3 * features, LANES):
            lanes = slice(lane, lane + LANES)
            total = total + w_ref[:, lanes].astype(jnp.float32) * qkv_ref[:, lanes]
        gain_ref[...] = jnp.sum(total.T, axis=0, keepdims=True) / scale_ref[...]

    return pl.pallas_call(
        body,
        out_shape=[
            jax.ShapeDtypeStruct((features, 3 * features), jnp.float32),
            jax.ShapeDtypeStruct((features, features), jnp.float32),
            jax.ShapeDtypeStruct((1, features), jnp.float32),
        ],
        in_specs=[pl.BlockSpec(memory_space=pltpu.VMEM)] * 3,
        out_specs=[pl.BlockSpec(memory_space=pltpu.VMEM)] * 3,
        scratch_shapes=[pltpu.VMEM((3 * features, features), jnp.bfloat16)],
        compiler_params=pltpu.CompilerParams(vmem_limit_bytes=8 << 20),
        name="unpack",
    )(whole, w_qkv, gain)


def in_hbm(array):
    return pltpu.with_memory_space_constraint(array, pltpu.HBM)


def per_device(tokens, d_out, gain, w_qkv, w_out, counts):
    features = tokens.shape[2]
    slot_count = tokens.shape[1] // WIN
    block = ("z_lo", "core", "help", "dp")
    gain = gain.reshape(1, features)
    grad_local, send = local_grads(
        in_hbm(counts),
        in_hbm(tokens[0].reshape(slot_count, WIN, features)),
        in_hbm(d_out[0].reshape(slot_count, WIN, features)),
        in_hbm(gain),
        in_hbm(w_qkv),
        in_hbm(w_out),
    )
    planes = lax.axis_size("z_hi")
    factor = 1.0 / math.sqrt(planes * lax.axis_size(block) * WKEEP * WIN)
    received = lax.all_to_all(send, block, 0, 0)
    copies = sum_copies(received, planes, 1.0, jnp.bfloat16)
    copies = sum_copies(lax.all_to_all(copies, "z_hi", 0, 0), PIECES, factor, jnp.bfloat16)
    grad_qkv, grad_out, grad_gain = unpack(lax.all_to_all(copies, block, 0, 0), w_qkv, gain)
    grad_tokens = grad_local.reshape(1, slot_count * WIN, features)
    return (grad_tokens, grad_qkv, grad_out, grad_gain.reshape(features))


def solution(mesh):
    shape = dict(mesh.shape)
    split = Mesh(
        mesh.devices.reshape(shape["tile"] // 4, 2, 2, shape["help"], shape["dp"]),
        ("z_hi", "z_lo", "core", "help", "dp"),
    )
    tile = ("z_hi", "z_lo", "core")
    in_specs = (
        P("dp", (*tile, "help"), None),
        P("dp", (*tile, "help"), None),
        P(),
        P(),
        P(),
        P("dp", tile),
    )
    out_specs = (P("dp", (*tile, "help"), None), P(), P(), P())
    return jax.shard_map(
        per_device, mesh=split, in_specs=in_specs, out_specs=out_specs, check_vma=False
    )
```
